32 devices in a mesh: row: 8 (over y, x, core), col: 4 (over z).
Axes of the slice: x: 2, y: 2, z: 4, core: 2. Of those that a mesh axis runs over, the one named last changes fastest.
Arguments:
- cam_jac: float32 [4, 2, 9, 4096], P(None, None, None, ('row', 'col')), may hold values from -0.6 to 0.6
- pt_jac: float32 [4, 2, 3, 4096], P(None, None, None, ('row', 'col')), may hold values from -6 to 6
- track_owner: int32 [4096, 4], P(('row', 'col')), may hold values from 0 to 31, all different within a row; in each aligned block of 128 rows (0 to 127, 128 to 255, ...) at most 32 rows name the same one
- track_cam: int32 [4096, 4], P(('row', 'col')), may hold values from 0 to 15
Outputs:
- reduced_system: float32 [4608, 4608], P(('row', 'col'))
The draws below stay inside these ranges and needn't reach their ends.
Inputs may be any that keep to these rules, and one draw needn't show every extreme that they name: `track_owner`: the 4 observations of a point lie in 4 different blocks. Among the points of one device no block is named by more than 32 observations.
All inputs are finite; a program needn't handle non-finite values.
Results may differ from the reference program's by a relative error of at most 0.0001.
Values sent between devices are 32-bit elements; how exact they have to be, the bound alone decides.
A program may use at most 128 MiB of HBM per device.

```python
import math
import jax
import jax.numpy as jnp
import numpy as np
from jax import lax

KOBS = 4
PTS_DEV = 128
CAM_DEV = 16
CAMERAS = 512
POINTS = 4096
CAP = 32
DEVICES = 32


def touch_ends(entries, stream_key, low, largest):
    longest = entries.shape.index(max(entries.shape))
    spots = []
    for shift in (0, 1):
        where = [jax.random.randint(jax.random.fold_in(stream_key, axis), (), 0, length) for axis, length in enumerate(entries.shape)]
        where[longest] = (where[longest] + shift) % entries.shape[longest]
        spots.append(tuple(where))
    return entries.at[spots[0]].set(low).at[spots[1]].set(largest)


def shard_levels(key, dims, pieces, least, high):
    level, own = 1.0, jax.random.fold_in(key, 6)
    for axis_at, blocks in pieces:
        heights = jnp.exp(jax.random.uniform(jax.random.fold_in(own, axis_at), (blocks,), jnp.float32, least / len(pieces), high / len(pieces)))
        level = level * jnp.repeat(heights, dims[axis_at] // blocks).reshape([-1 if axis == axis_at else 1 for axis in range(len(dims))])
    return level


def deal_out(own_key, own, number, rows, amount, top, limit, lean):
    ranking = jax.random.permutation(own_key, amount)
    heavy_load, usual = load_shares(amount, rows * top, limit, lean, True), load_shares(amount, rows * top, limit, lean, False)
    places = jnp.arange(amount)

    def named(sizes, offset_by):
        used = int((sizes > 0).sum())
        fixed = max(1, used // 4)
        shifted = fixed + (places - fixed + offset_by * (used - fixed)) % max(1, amount - fixed)
        return jnp.zeros((amount,), jnp.int32).at[ranking[jnp.where(places < fixed, places, shifted)]].set(jnp.asarray(sizes, jnp.int32))

    sizes = jnp.where(number % 4 == 0, named(heavy_load, number // 4), named(usual, number - number // 4 - 1))
    mixed = jax.random.permutation(jax.random.fold_in(own, 3), amount)
    donor, taker = mixed[0:amount // 2 * 2:2], mixed[1:amount // 2 * 2:2]
    slack = jnp.minimum(sizes[donor] - 1, limit - sizes[taker]) // 2
    slack = jnp.where((donor == ranking[0]) | (taker == ranking[0]) | (sizes[taker] == 0), 0, jnp.maximum(slack, 0))
    shifted = jax.random.randint(jax.random.fold_in(own, 4), (amount // 2,), 0, 1 << 20) % (slack + 1)
    sizes = sizes.at[donor].add(-shifted).at[taker].add(shifted)
    labels = jnp.searchsorted(jnp.cumsum(sizes), jnp.arange(rows * top), side="right").astype(jnp.int32)
    listing = labels.reshape(top, rows).T
    listing = listing[jax.random.permutation(jax.random.fold_in(own, 1), rows)]
    offset_by = jax.random.randint(jax.random.fold_in(own, 2), (rows, 1), 0, top)
    return jnp.take_along_axis(listing, (jnp.arange(top)[None, :] + offset_by) % top, axis=1)


def load_shares(number_of, total, most, skew, full):
    loads = [(1 << 20) // math.isqrt(standing ** skew) + 1 for standing in range(1, number_of + 1)]
    largest = most if full else min(most, max(-(-total // number_of), total * loads[0] // sum(loads)))
    least = 1 if total - largest >= number_of - 1 else 0
    given, surplus = [largest] + [least] * (number_of - 1), total - largest - least * (number_of - 1)
    while surplus > 0:
        candidates = [i for i in range(1, number_of) if given[i] < largest] or [i for i in range(1, number_of) if given[i] < most]
        pool, left = sum([loads[i] for i in candidates]), surplus
        for i in candidates:
            addition = min(most - given[i], max(1, left * loads[i] // pool), surplus)
            given[i] = given[i] + addition
            surplus = surplus - addition
    return np.array(given)


def gaussian(rng, shape, width, reach, split=(), held_as=jnp.bfloat16):
    level = shard_levels(rng, shape, split, -0.22, 0.18) if split else 1.0
    entries = jax.random.normal(rng, shape, jnp.float32) * width * level
    return jnp.minimum(jnp.maximum(entries, -reach), reach).astype(held_as)


def setup_inputs(seed: int = 0) -> dict:
    splits = jax.random.split(jax.random.key(seed), 5)
    cam_jac = gaussian(splits[0], (KOBS, 2, 9, POINTS), 0.1, 0.6, ((3, 32),), jnp.float32)
    pt_jac = gaussian(splits[1], (KOBS, 2, 3, POINTS), 1.0, 6.0, ((3, 32),), jnp.float32)
    track_owner_keys = jax.random.split(jax.random.fold_in(splits[2], 1), POINTS // PTS_DEV)
    track_owner_turns = jax.random.permutation(jax.random.fold_in(splits[2], 3), POINTS // PTS_DEV)
    track_owner = jax.vmap(lambda own, number: deal_out(jax.random.fold_in(splits[2], 2), own, number, PTS_DEV, DEVICES, KOBS, CAP, 2))(track_owner_keys, track_owner_turns).reshape((POINTS, KOBS))
    track_cam = touch_ends(jax.random.randint(splits[3], (POINTS, KOBS), 0, CAM_DEV), jax.random.fold_in(splits[3], 1), 0, CAM_DEV - 1).astype(jnp.int32)
    return {"cam_jac": cam_jac, "pt_jac": pt_jac, "track_owner": track_owner, "track_cam": track_cam}


point_damping = 1.0

def eliminate(cam_jac, pt_jac):
    exact_precision = lax.Precision.HIGHEST
    normal = jnp.einsum('ktin,ktjn->ijn', pt_jac, pt_jac, precision=exact_precision)
    pivot_first = jnp.sqrt(normal[0, 0] + point_damping)
    below_first = normal[1, 0] / pivot_first
    below_second = normal[2, 0] / pivot_first
    pivot_second = jnp.sqrt(normal[1, 1] + point_damping - below_first * below_first)
    below_middle = (normal[2, 1] - below_second * below_first) / pivot_second
    pivot_third = jnp.sqrt(normal[2, 2] + point_damping - below_second * below_second - below_middle * below_middle)
    coupled = jnp.einsum('ktpn,ktrn->kprn', cam_jac, pt_jac, precision=exact_precision)
    column_first = coupled[:, :, 0] / pivot_first
    column_second = (coupled[:, :, 1] - column_first * below_first) / pivot_second
    third_column_block = (coupled[:, :, 2] - column_first * below_second - column_second * below_middle) / pivot_third
    return jnp.stack([column_first, column_second, third_column_block], axis=2)

def reference(cam_jac, pt_jac, track_owner, track_cam):
    exact_precision = lax.Precision.HIGHEST
    camera = (track_owner * CAM_DEV + track_cam).astype(jnp.int32)
    eliminated = jnp.transpose(eliminate(cam_jac, pt_jac), (3, 0, 1, 2))
    camera_row_blocks = jnp.transpose(cam_jac, (3, 0, 1, 2))
    system = jnp.zeros((CAMERAS, CAMERAS, 9, 9), jnp.float32)
    for first_obs in range(KOBS):
        for second_obs in range(KOBS):
            block_terms = -jnp.einsum('npr,nqr->npq', eliminated[:, first_obs], eliminated[:, second_obs], precision=exact_precision)
            if first_obs == second_obs:
                block_terms = block_terms + jnp.einsum('ntp,ntq->npq', camera_row_blocks[:, first_obs], camera_row_blocks[:, first_obs], precision=exact_precision)
            system = system.at[camera[:, first_obs], camera[:, second_obs]].add(block_terms)
    return jnp.transpose(system, (0, 2, 1, 3)).reshape(9 * CAMERAS, 9 * CAMERAS)
```

```python
import functools
import jax
import jax.numpy as jnp
from jax import lax
from jax.experimental import pallas as pl
from jax.experimental.pallas import tpu as pltpu
from jax.sharding import PartitionSpec as P

CAM_TILE = 64
GROUP = 128
point_damping = 1.0
NT = (((1,), (1,)), ((), ()))
NN = (((1,), (0,)), ((), ()))


def split(x):
    high = x.astype(jnp.bfloat16)
    return high, (x - high.astype(jnp.float32)).astype(jnp.bfloat16)


def dot(a, b, dims):
    return lax.dot_general(a, b, dims, preferred_element_type=jnp.float32)


def assemble(obs, cams_device, me_ref, got_ref, out_ref,
             lhs_ref, elim_ref, rhs_ref, perm_ref, ids_ref, own_ref):
    step = pl.program_id(0)
    total = got_ref.shape[0]
    rows = cams_device * 9
    owners = GROUP // cams_device
    me = me_ref[0]
    first = me * cams_device

    @pl.when(step == 0)
    def _():
        feats = jnp.transpose(got_ref[...])
        cam = [[feats[(k * 2 + t) * 9:(k * 2 + t) * 9 + 9] for t in range(2)] for k in range(obs)]
        base = obs * 18
        pt = [[[feats[base + (k * 2 + t) * 3 + r:base + (k * 2 + t) * 3 + r + 1]
                for r in range(3)] for t in range(2)] for k in range(obs)]
        ids = feats[base + obs * 6:base + obs * 7].astype(jnp.int32)
        ids_ref[:obs] = ids

        def normal(i, j):
            return sum(pt[k][t][i] * pt[k][t][j] for k in range(obs) for t in range(2))

        pivot_first = jnp.sqrt(normal(0, 0) + point_damping)
        below_first = normal(1, 0) / pivot_first
        below_second = normal(2, 0) / pivot_first
        pivot_second = jnp.sqrt(normal(1, 1) + point_damping - below_first * below_first)
        below_middle = (normal(2, 1) - below_second * below_first) / pivot_second
        pivot_third = jnp.sqrt(normal(2, 2) + point_damping - below_second * below_second
                               - below_middle * below_middle)
        elim = []
        for k in range(obs):
            coupled = [cam[k][0] * pt[k][0][r] + cam[k][1] * pt[k][1][r] for r in range(3)]
            one = coupled[0] / pivot_first
            two = (coupled[1] - one * below_first) / pivot_second
            three = (coupled[2] - one * below_second - two * below_middle) / pivot_third
            elim.append([one, two, three])
            high, low = split(jnp.concatenate([one, two, three], axis=0))
            elim_ref[0, k] = high.astype(jnp.float32)
            elim_ref[1, k] = low.astype(jnp.float32)

        mine = [(ids[k:k + 1] >= first) & (ids[k:k + 1] < first + cams_device) for k in range(obs)]
        place = jnp.zeros((1, total), jnp.int32)
        for k in range(obs):
            place = jnp.where(mine[k], ids[k:k + 1] - first, place)
        owner_row = lax.broadcasted_iota(jnp.int32, (rows, total), 0) // 9
        spread = (lax.broadcasted_iota(jnp.int32, (rows, 16), 0) % 9
                  == lax.broadcasted_iota(jnp.int32, (rows, 16), 1)).astype(jnp.bfloat16)
        keep = owner_row == place

        def tiled(piece):
            pad = jnp.concatenate([piece, jnp.zeros((7, total), jnp.float32)], axis=0)
            high, low = split(pad)
            return [jnp.where(keep, dot(spread, part, NN), 0.0).astype(jnp.bfloat16)
                    for part in (high, low)]

        for r in range(3):
            anchor = sum(jnp.where(mine[k], elim[k][r], 0.0) for k in range(obs))
            high, low = tiled(-anchor)
            lhs_ref[:rows, r * total:(r + 1) * total] = high
            lhs_ref[rows:, r * total:(r + 1) * total] = low

        diag = jnp.zeros((rows, rows), jnp.float32)
        for t in range(2):
            anchor = sum(jnp.where(mine[k], cam[k][t], 0.0) for k in range(obs))
            high, low = tiled(anchor)
            both = dot(jnp.concatenate([high, low], axis=0), high, NT)
            diag = diag + both[:rows] + both[rows:] + dot(high, low, NT)
        same = (lax.broadcasted_iota(jnp.int32, (rows, rows), 0) // 9
                == lax.broadcasted_iota(jnp.int32, (rows, rows), 1) // 9)
        own_ref[...] = jnp.where(same, diag, 0.0)

        source = lax.broadcasted_iota(jnp.int32, (9 * GROUP, 1), 0)
        goal = (source % GROUP) * 9 + source // GROUP
        perm_ref[...] = (lax.broadcasted_iota(jnp.int32, (9 * GROUP, 9 * GROUP), 1) == goal
                         ).astype(jnp.bfloat16)

    cam_row = lax.broadcasted_iota(jnp.int32, (cams_device, total), 0)

    for j in range(owners):
        start = step * GROUP + j * cams_device
        ids = ids_ref[:obs]
        named = [(ids[k:k + 1] >= start) & (ids[k:k + 1] < start + cams_device) for k in range(obs)]
        place = jnp.full((1, total), -1, jnp.int32)
        for k in range(obs):
            place = jnp.where(named[k], ids[k:k + 1] - start, place)
        mask = cam_row == place
        for part in range(2):
            chosen = jnp.zeros((27, total), jnp.float32)
            for k in range(obs):
                chosen = jnp.where(named[k], elim_ref[part, k], chosen)
            for r in range(3):
                for q in range(9):
                    at = q * GROUP + j * cams_device
                    rhs_ref[part, at:at + cams_device, r * total:(r + 1) * total] = jnp.where(
                        mask, chosen[r * 9 + q:r * 9 + q + 1], 0.0).astype(jnp.bfloat16)

    both = dot(lhs_ref[...], rhs_ref[0], NT)
    block = both[:rows] + both[rows:] + dot(lhs_ref[:rows], rhs_ref[1], NT)
    high, low = split(block)
    both = dot(jnp.concatenate([high, low], axis=0), perm_ref[...], NN)
    out_ref[...] = both[:rows] + both[rows:]

    @pl.when(me // owners == step)
    def _():
        put = (lax.broadcasted_iota(jnp.int32, (rows, 9 * GROUP), 1)
               == lax.broadcasted_iota(jnp.int32, (rows, 9 * GROUP), 0)
               + (me % owners) * rows).astype(jnp.bfloat16)
        high, low = split(own_ref[...])
        out_ref[...] += dot(high, put, NN) + dot(low, put, NN)


def shards(cam_jac, pt_jac, track_owner, track_cam):
    obs = cam_jac.shape[0]
    points = cam_jac.shape[3]
    device_count = lax.axis_size("row") * lax.axis_size("col")
    cams_device = CAM_TILE // lax.axis_size("col")
    slots = 2 * points * obs // device_count
    rows = cams_device * 9
    total = device_count * slots

    camera = track_owner * cams_device + track_cam
    data = jnp.concatenate([
        cam_jac.reshape(obs * 18, points),
        pt_jac.reshape(obs * 6, points),
        jnp.transpose(camera).astype(jnp.float32),
        jnp.zeros((128 - obs * 25, points), jnp.float32),
    ], axis=0)
    devices = jnp.arange(device_count, dtype=jnp.int32)
    names = jnp.any(track_owner[:, :, None] == devices, axis=1)
    earlier = jnp.tril(jnp.ones((points, points), jnp.bfloat16), -1)
    rank = jnp.einsum("mn,nd->dm", earlier, names.astype(jnp.bfloat16),
                      preferred_element_type=jnp.float32)
    pick = jnp.where(
        names.T[:, None, :]
        & (rank[:, None, :] == jnp.arange(slots, dtype=jnp.float32)[None, :, None]), 1.0, 0.0)
    send = lax.dot_general(pick.reshape(total, points), data, NT,
                           precision=lax.Precision.HIGHEST,
                           preferred_element_type=jnp.float32)
    got = lax.all_to_all(send.reshape(device_count, slots, 128), ("row", "col"),
                         split_axis=0, concat_axis=0, tiled=True).reshape(total, 128)
    me = lax.axis_index(("row", "col")).astype(jnp.int32).reshape(1)
    steps = device_count * cams_device // GROUP
    return pl.pallas_call(
        functools.partial(assemble, obs, cams_device),
        grid=(steps,),
        out_shape=jax.ShapeDtypeStruct((rows, device_count * rows), jnp.float32),
        in_specs=[pl.BlockSpec(memory_space=pltpu.SMEM),
                  pl.BlockSpec((total, 128), lambda i: (0, 0))],
        out_specs=pl.BlockSpec((rows, 9 * GROUP), lambda i: (0, i)),
        scratch_shapes=[
            pltpu.VMEM((2 * rows, 3 * total), jnp.bfloat16),
            pltpu.VMEM((2, obs, 27, total), jnp.float32),
            pltpu.VMEM((2, 9 * GROUP, 3 * total), jnp.bfloat16),
            pltpu.VMEM((9 * GROUP, 9 * GROUP), jnp.bfloat16),
            pltpu.VMEM((8, total), jnp.int32),
            pltpu.VMEM((rows, rows), jnp.float32),
        ],
        compiler_params=pltpu.CompilerParams(
            dimension_semantics=("arbitrary",), vmem_limit_bytes=60 * 1024 * 1024),
    )(me, got)


def solution(mesh):
    placed = (
        P(None, None, None, ("row", "col")),
        P(None, None, None, ("row", "col")),
        P(("row", "col"), None),
        P(("row", "col"), None),
    )
    return jax.shard_map(
        shards, mesh=mesh, in_specs=placed, out_specs=P(("row", "col"), None), check_vma=False
    )
```

```python
import functools
import jax
import jax.numpy as jnp
from jax import lax
from jax.experimental import pallas as pl
from jax.experimental.pallas import tpu as pltpu
from jax.sharding import PartitionSpec as P

CAM_TILE = 64
GROUP = 128
point_damping = 1.0
NT = (((1,), (1,)), ((), ()))
NN = (((1,), (0,)), ((), ()))


def split(x):
    high = x.astype(jnp.bfloat16)
    return high, (x - high.astype(jnp.float32)).astype(jnp.bfloat16)


def dot(a, b, dims):
    return lax.dot_general(a, b, dims, preferred_element_type=jnp.float32)


def assemble(obs, cams_device, me_ref, got_ref, out_ref,
             lhs_ref, elim_ref, rhs_ref, perm_ref, ids_ref, own_ref):
    step = pl.program_id(0)
    total = got_ref.shape[0]
    rows = cams_device * 9
    owners = GROUP // cams_device
    me = me_ref[0]
    first = me * cams_device

    @pl.when(step == 0)
    def _():
        feats = jnp.transpose(got_ref[...])
        cam = [[feats[(k * 2 + t) * 9:(k * 2 + t) * 9 + 9] for t in range(2)] for k in range(obs)]
        base = obs * 18
        pt = [[[feats[base + (k * 2 + t) * 3 + r:base + (k * 2 + t) * 3 + r + 1]
                for r in range(3)] for t in range(2)] for k in range(obs)]
        ids = feats[base + obs * 6:base + obs * 7].astype(jnp.int32)
        ids_ref[:obs] = ids

        def normal(i, j):
            return sum(pt[k][t][i] * pt[k][t][j] for k in range(obs) for t in range(2))

        pivot_first = jnp.sqrt(normal(0, 0) + point_damping)
        below_first = normal(1, 0) / pivot_first
        below_second = normal(2, 0) / pivot_first
        pivot_second = jnp.sqrt(normal(1, 1) + point_damping - below_first * below_first)
        below_middle = (normal(2, 1) - below_second * below_first) / pivot_second
        pivot_third = jnp.sqrt(normal(2, 2) + point_damping - below_second * below_second
                               - below_middle * below_middle)
        elim = []
        for k in range(obs):
            coupled = [cam[k][0] * pt[k][0][r] + cam[k][1] * pt[k][1][r] for r in range(3)]
            one = coupled[0] / pivot_first
            two = (coupled[1] - one * below_first) / pivot_second
            three = (coupled[2] - one * below_second - two * below_middle) / pivot_third
            elim.append([one, two, three])
            high, low = split(jnp.concatenate([one, two, three], axis=0))
            elim_ref[0, k] = high.astype(jnp.float32)
            elim_ref[1, k] = low.astype(jnp.float32)

        mine = [(ids[k:k + 1] >= first) & (ids[k:k + 1] < first + cams_device) for k in range(obs)]
        place = jnp.zeros((1, total), jnp.int32)
        for k in range(obs):
            place = jnp.where(mine[k], ids[k:k + 1] - first, place)
        owner_row = lax.broadcasted_iota(jnp.int32, (rows, total), 0) // 9
        spread = (lax.broadcasted_iota(jnp.int32, (rows, 16), 0) % 9
                  == lax.broadcasted_iota(jnp.int32, (rows, 16), 1)).astype(jnp.bfloat16)
        keep = owner_row == place

        def tiled(piece):
            pad = jnp.concatenate([piece, jnp.zeros((7, total), jnp.float32)], axis=0)
            high, low = split(pad)
            return [jnp.where(keep, dot(spread, part, NN), 0.0).astype(jnp.bfloat16)
                    for part in (high, low)]

        for r in range(3):
            anchor = sum(jnp.where(mine[k], elim[k][r], 0.0) for k in range(obs))
            high, low = tiled(-anchor)
            lhs_ref[:rows, r * total:(r + 1) * total] = high
            lhs_ref[rows:, r * total:(r + 1) * total] = low

        diag = jnp.zeros((rows, rows), jnp.float32)
        for t in range(2):
            anchor = sum(jnp.where(mine[k], cam[k][t], 0.0) for k in range(obs))
            high, low = tiled(anchor)
            both = dot(jnp.concatenate([high, low], axis=0), high, NT)
            diag = diag + both[:rows] + both[rows:] + dot(high, low, NT)
        same = (lax.broadcasted_iota(jnp.int32, (rows, rows), 0) // 9
                == lax.broadcasted_iota(jnp.int32, (rows, rows), 1) // 9)
        own_ref[...] = jnp.where(same, diag, 0.0)

        source = lax.broadcasted_iota(jnp.int32, (9 * GROUP, 1), 0)
        goal = (source % GROUP) * 9 + source // GROUP
        perm_ref[...] = (lax.broadcasted_iota(jnp.int32, (9 * GROUP, 9 * GROUP), 1) == goal
                         ).astype(jnp.bfloat16)

    cam_row = lax.broadcasted_iota(jnp.int32, (cams_device, total), 0)

    for j in range(owners):
        start = step * GROUP + j * cams_device
        ids = ids_ref[:obs]
        named = [(ids[k:k + 1] >= start) & (ids[k:k + 1] < start + cams_device) for k in range(obs)]
        place = jnp.full((1, total), -1, jnp.int32)
        for k in range(obs):
            place = jnp.where(named[k], ids[k:k + 1] - start, place)
        mask = cam_row == place
        for part in range(2):
            chosen = jnp.zeros((27, total), jnp.float32)
            for k in range(obs):
                chosen = jnp.where(named[k], elim_ref[part, k], chosen)
            for r in range(3):
                for q in range(9):
                    at = q * GROUP + j * cams_device
                    rhs_ref[part, at:at + cams_device, r * total:(r + 1) * total] = jnp.where(
                        mask, chosen[r * 9 + q:r * 9 + q + 1], 0.0).astype(jnp.bfloat16)

    both = dot(lhs_ref[...], rhs_ref[0], NT)
    block = both[:rows] + both[rows:] + dot(lhs_ref[:rows], rhs_ref[1], NT)
    high, low = split(block)
    both = dot(jnp.concatenate([high, low], axis=0), perm_ref[...], NN)
    out_ref[...] = both[:rows] + both[rows:]

    @pl.when(me // owners == step)
    def _():
        put = (lax.broadcasted_iota(jnp.int32, (rows, 9 * GROUP), 1)
               == lax.broadcasted_iota(jnp.int32, (rows, 9 * GROUP), 0)
               + (me % owners) * rows).astype(jnp.bfloat16)
        high, low = split(own_ref[...])
        out_ref[...] += dot(high, put, NN) + dot(low, put, NN)


def exchange(count, cols, send_ref, out_ref, got_ref, send_sem, recv_sem):
    me = lax.axis_index("row") * cols + lax.axis_index("col")
    barrier = pltpu.get_barrier_semaphore()

    def spot(shift):
        peer = lax.rem(me + shift, count)
        return peer, (lax.div(peer, cols), lax.rem(peer, cols))

    for shift in range(1, count):
        pl.semaphore_signal(barrier, inc=1, device_id=spot(shift)[1],
                            device_id_type=pl.DeviceIdType.MESH)
    pl.semaphore_wait(barrier, count - 1)
    copies = []
    for shift in range(1, count):
        peer, where = spot(shift)
        copy = pltpu.make_async_remote_copy(
            src_ref=send_ref.at[peer],
            dst_ref=got_ref.at[shift],
            send_sem=send_sem.at[shift],
            recv_sem=recv_sem.at[shift],
            device_id=where,
            device_id_type=pl.DeviceIdType.MESH,
        )
        copy.start()
        copies.append(copy)
    out_ref[0] = send_ref[me]
    for copy in copies:
        copy.wait()
    for shift in range(1, count):
        out_ref[shift] = got_ref[shift]


def shards(cam_jac, pt_jac, track_owner, track_cam):
    obs = cam_jac.shape[0]
    points = cam_jac.shape[3]
    device_count = lax.axis_size("row") * lax.axis_size("col")
    cams_device = CAM_TILE // lax.axis_size("col")
    slots = 2 * points * obs // device_count
    rows = cams_device * 9
    total = device_count * slots

    camera = track_owner * cams_device + track_cam
    data = jnp.concatenate([
        cam_jac.reshape(obs * 18, points),
        pt_jac.reshape(obs * 6, points),
        jnp.transpose(camera).astype(jnp.float32),
        jnp.zeros((128 - obs * 25, points), jnp.float32),
    ], axis=0)
    devices = jnp.arange(device_count, dtype=jnp.int32)
    names = jnp.any(track_owner[:, :, None] == devices, axis=1)
    earlier = jnp.tril(jnp.ones((points, points), jnp.bfloat16), -1)
    rank = jnp.einsum("mn,nd->dm", earlier, names.astype(jnp.bfloat16),
                      preferred_element_type=jnp.float32)
    pick = jnp.where(
        names.T[:, None, :]
        & (rank[:, None, :] == jnp.arange(slots, dtype=jnp.float32)[None, :, None]), 1.0, 0.0)
    send = lax.dot_general(pick.reshape(total, points), data, NT,
                           precision=lax.Precision.HIGHEST,
                           preferred_element_type=jnp.float32)
    block = (device_count, slots, 128)
    got = pl.pallas_call(
        functools.partial(exchange, device_count, lax.axis_size("col")),
        out_shape=jax.ShapeDtypeStruct(block, jnp.float32),
        in_specs=[pl.BlockSpec(memory_space=pltpu.VMEM)],
        out_specs=pl.BlockSpec(memory_space=pltpu.VMEM),
        scratch_shapes=[
            pltpu.VMEM(block, jnp.float32),
            pltpu.SemaphoreType.DMA((device_count,)),
            pltpu.SemaphoreType.DMA((device_count,)),
        ],
        compiler_params=pltpu.CompilerParams(collective_id=0, has_side_effects=True),
    )(send.reshape(block)).reshape(total, 128)
    me = lax.axis_index(("row", "col")).astype(jnp.int32).reshape(1)
    steps = device_count * cams_device // GROUP
    return pl.pallas_call(
        functools.partial(assemble, obs, cams_device),
        grid=(steps,),
        out_shape=jax.ShapeDtypeStruct((rows, device_count * rows), jnp.float32),
        in_specs=[pl.BlockSpec(memory_space=pltpu.SMEM),
                  pl.BlockSpec((total, 128), lambda i: (0, 0))],
        out_specs=pl.BlockSpec((rows, 9 * GROUP), lambda i: (0, i)),
        scratch_shapes=[
            pltpu.VMEM((2 * rows, 3 * total), jnp.bfloat16),
            pltpu.VMEM((2, obs, 27, total), jnp.float32),
            pltpu.VMEM((2, 9 * GROUP, 3 * total), jnp.bfloat16),
            pltpu.VMEM((9 * GROUP, 9 * GROUP), jnp.bfloat16),
            pltpu.VMEM((8, total), jnp.int32),
            pltpu.VMEM((rows, rows), jnp.float32),
        ],
        compiler_params=pltpu.CompilerParams(
            dimension_semantics=("arbitrary",), vmem_limit_bytes=60 * 1024 * 1024),
    )(me, got)


def solution(mesh):
    placed = (
        P(None, None, None, ("row", "col")),
        P(None, None, None, ("row", "col")),
        P(("row", "col"), None),
        P(("row", "col"), None),
    )
    return jax.shard_map(
        shards, mesh=mesh, in_specs=placed, out_specs=P(("row", "col"), None), check_vma=False
    )
```
